32 devices in a mesh: expert: 4 (over z), dp: 8 (over y, x, core).
Axes of the slice: x: 2, y: 2, z: 4, core: 2. Of those that a mesh axis runs over, the one named last changes fastest.
Arguments:
- tokens: bfloat16 [1024, 1408], P('dp', 'expert'), may hold values from -6 to 6
- routes: int32 [1024, 2], P('dp'), may hold values from 0 to 7, all different within a row; in each aligned block of 128 rows (0 to 127, 128 to 255, ...) at most 40 rows name the same one
- gate_values: float32 [1024, 2], P('dp'), may hold values from 0.2 to 1
- expert_in: bfloat16 [8, 1408, 6144], P('expert', None, 'dp'), may hold values from -0.15625 to 0.15625
- expert_out: bfloat16 [8, 6144, 1408], P('expert', 'dp'), may hold values from -0.078125 to 0.078125
- cotangent: bfloat16 [1024, 1408], P('dp', 'expert'), may hold values from -1.1953125 to 1.1953125
Outputs:
- layer_out: bfloat16 [1024, 1408], P('dp', 'expert')
- grad_tokens: bfloat16 [1024, 1408], P('dp', 'expert')
- grad_gates: float32 [1024, 2], P('dp')
- grad_in: bfloat16 [8, 1408, 6144], P('expert', None, 'dp')
- grad_out: bfloat16 [8, 6144, 1408], P('expert', 'dp')
The draws below stay inside these ranges and needn't reach their ends.
Inputs may be any that keep to these rules, and one draw needn't show every extreme that they name: `routes`: each row names two different experts. In each aligned block of 128 rows no expert is named by more than 40 rows, a bound that some block reaches.
All inputs are finite; a program needn't handle non-finite values.
Results may differ from the reference program's by a relative error of at most 0.014.
Values may be sent and summed in bfloat16 or wider, within the bound.
A program may use at most 128 MiB of HBM per device.

```python
import math
import jax
import jax.numpy as jnp
import numpy as np
from jax import lax

D = 1408
FF = 6144
TOK_DEV = 128
EXPERTS = 8
CAP = 40
TOKENS = 1024
N_DP = 8


def block_scale(key, shape, pieces, low, largest):
    factor_of = 1.0
    for position, shards_of in pieces:
        heights = jax.random.uniform(jax.random.fold_in(jax.random.fold_in(key, 6), position), (shards_of,), jnp.float32, low / len(pieces), largest / len(pieces))
        factor_of = factor_of * jnp.repeat(jnp.exp(heights), shape[position] // shards_of).reshape((-1,) + (1,) * (len(shape) - 1 - position))
    return factor_of


def routed_block(rng, own, number, rows, amount, top, bound, lean):
    sequence = jax.random.permutation(rng, amount)
    crowded, usual = shares(amount, rows * top, bound, lean, True), shares(amount, rows * top, bound, lean, False)
    places = jnp.arange(amount)

    def named(sizes, rotation):
        used = int((sizes > 0).sum())
        fixed = max(1, used // 4)
        moved = fixed + (places - fixed + rotation * (used - fixed)) % max(1, amount - fixed)
        return jnp.zeros((amount,), jnp.int32).at[sequence[jnp.where(places < fixed, places, moved)]].set(jnp.asarray(sizes, jnp.int32))

    sizes = jnp.where(number % 4 == 0, named(crowded, number // 4), named(usual, number - number // 4 - 1))
    mixed = jax.random.permutation(jax.random.fold_in(own, 3), amount)
    giver, sink = mixed[0:amount // 2 * 2:2], mixed[1:amount // 2 * 2:2]
    margin = jnp.minimum(sizes[giver] - 1, bound - sizes[sink]) // 2
    margin = jnp.where((giver == sequence[0]) | (sink == sequence[0]) | (sizes[sink] == 0), 0, jnp.maximum(margin, 0))
    moved = jax.random.randint(jax.random.fold_in(own, 4), (amount // 2,), 0, 1 << 20) % (margin + 1)
    sizes = sizes.at[giver].add(-moved).at[sink].add(moved)
    members = jnp.searchsorted(jnp.cumsum(sizes), jnp.arange(rows * top), side="right").astype(jnp.int32)
    table = members.reshape(top, rows).T
    table = table[jax.random.permutation(jax.random.fold_in(own, 1), rows)]
    rotation = jax.random.randint(jax.random.fold_in(own, 2), (rows, 1), 0, top)
    return jnp.take_along_axis(table, (jnp.arange(top)[None, :] + rotation) % top, axis=1)


def shares(number_of, total, most, slope, full):
    weights = [(1 << 20) // math.isqrt(rank ** slope) + 1 for rank in range(1, number_of + 1)]
    largest = most if full else min(most, max(-(-total // number_of), total * weights[0] // sum(weights)))
    least = 1 if total - largest >= number_of - 1 else 0
    counts, spare = [largest] + [least] * (number_of - 1), total - largest - least * (number_of - 1)
    while spare > 0:
        movable = [i for i in range(1, number_of) if counts[i] < largest] or [i for i in range(1, number_of) if counts[i] < most]
        whole, left = sum([weights[i] for i in movable]), spare
        for i in movable:
            more = min(most - counts[i], max(1, left * weights[i] // whole), spare)
            counts[i] = counts[i] + more
            spare = spare - more
    return np.array(counts)


def normal_values(key, extent, width, bound, shards=(), held_as=jnp.bfloat16):
    entries = width * jax.random.normal(key, extent, jnp.float32)
    if shards:
        entries = entries * block_scale(key, extent, shards, -0.22, 0.18)
    return jnp.clip(entries, -bound, bound).astype(held_as)


def setup_inputs(seed: int = 0) -> dict:
    seeds = jax.random.split(jax.random.key(seed), 7)
    tokens = normal_values(seeds[0], (TOKENS, D), 1.0, 6.0, ((0, 8), (1, 4)))
    routes_keys = jax.random.split(jax.random.fold_in(seeds[1], 1), TOKENS // TOK_DEV)
    routes_turns = jax.random.permutation(jax.random.fold_in(seeds[1], 3), TOKENS // TOK_DEV)
    routes = jax.vmap(lambda own, number: routed_block(jax.random.fold_in(seeds[1], 2), own, number, TOK_DEV, EXPERTS, 2, CAP, 2))(routes_keys, routes_turns).reshape((TOKENS, 2))
    gate_values = jnp.clip(0.2 + 0.8 * jax.random.uniform(seeds[2], (TOKENS, 2), jnp.float32) ** block_scale(seeds[2], (TOKENS, 2), ((0, 8),), -0.2, 0.2), 0.2, 1.0)
    expert_in = normal_values(seeds[3], (EXPERTS, D, FF), D ** -0.5, 0.15625, ((0, 4), (2, 8)))
    expert_out = normal_values(seeds[4], (EXPERTS, FF, D), FF ** -0.5, 0.078125, ((0, 4), (1, 8)))
    cotangent = normal_values(seeds[5], (TOKENS, D), 0.2, 1.1953125, ((0, 8), (1, 4)))
    return dict(tokens=tokens, routes=routes, gate_values=gate_values, expert_in=expert_in, expert_out=expert_out, cotangent=cotangent)


def gelu_tanh(values):
    return jax.nn.gelu(values, approximate=True)

def slot_table(routes):
    blocks = routes.reshape(N_DP, TOK_DEV * 2).astype(jnp.int32)
    onehot = (blocks[:, :, None] == jnp.arange(EXPERTS, dtype=jnp.int32)[None, None, :]).astype(jnp.int32)
    earlier = jnp.cumsum(onehot, axis=1, dtype=jnp.int32) - onehot
    rank_in = lax.optimization_barrier(jnp.sum(earlier * onehot, axis=2)).astype(jnp.int32)
    return (blocks * CAP + rank_in).astype(jnp.int32)

def place(pairs, table):

    def one_block(values, slots):
        return jnp.zeros((EXPERTS * CAP, D), jnp.bfloat16).at[slots].set(values)
    return jax.vmap(one_block)(pairs, table)

def grouped(left, right):
    rows_here = left.shape[0]
    left_parts = left.astype(jnp.float32).reshape(rows_here, N_DP, FF // N_DP)
    right_parts = right.astype(jnp.float32).reshape(N_DP, FF // N_DP, D)
    partial_sums = jnp.einsum('rgf,gfd->grd', left_parts, right_parts, precision=lax.Precision.HIGHEST)
    rounded = lax.optimization_barrier(partial_sums.astype(jnp.bfloat16))
    return lax.optimization_barrier(jnp.sum(rounded.astype(jnp.float32), axis=0)).astype(jnp.bfloat16)

def expert_pass(operands):
    x_rows, dy_rows, weight_in, weight_out = operands
    pre_act = jnp.dot(x_rows, weight_in, preferred_element_type=jnp.float32)
    hidden = gelu_tanh(pre_act).astype(jnp.bfloat16)
    d_hidden = jnp.dot(dy_rows, weight_out.T, preferred_element_type=jnp.float32)
    d_pre = jax.vjp(gelu_tanh, pre_act)[1](d_hidden)[0].astype(jnp.bfloat16)
    grad_out = jnp.dot(hidden.T, dy_rows, preferred_element_type=jnp.float32).astype(jnp.bfloat16)
    grad_in = jnp.dot(x_rows.T, d_pre, preferred_element_type=jnp.float32).astype(jnp.bfloat16)
    return (grouped(hidden, weight_out), grouped(d_pre, weight_in.T), grad_in, grad_out)

def by_expert(slots):
    return slots.reshape(N_DP, EXPERTS, CAP, D).transpose(1, 0, 2, 3).reshape(EXPERTS, N_DP * CAP, D)

def by_block(per_expert):
    return per_expert.reshape(EXPERTS, N_DP, CAP, D).transpose(1, 0, 2, 3).reshape(N_DP, EXPERTS * CAP, D)

def pick(arrays, table):
    return jax.vmap(lambda block, slots: block[slots])(arrays, table)

def reference(tokens, routes, gate_values, expert_in, expert_out, cotangent):
    table = slot_table(routes)
    gates = gate_values.reshape(N_DP, TOK_DEV * 2).astype(jnp.float32)
    pair_x = jnp.repeat(tokens.reshape(N_DP, TOK_DEV, D), 2, axis=1)
    cot_blocks = cotangent.reshape(N_DP, TOK_DEV, D).astype(jnp.float32)
    pair_dy = (jnp.repeat(cot_blocks, 2, axis=1) * gates[:, :, None]).astype(jnp.bfloat16)
    outputs, input_grads, grad_in, grad_out = lax.map(expert_pass, (by_expert(place(pair_x, table)), by_expert(place(pair_dy, table)), expert_in, expert_out))
    out_pairs = pick(by_block(outputs), table).astype(jnp.float32).reshape(N_DP, TOK_DEV, 2, D)
    dx_pairs = pick(by_block(input_grads), table).astype(jnp.float32).reshape(N_DP, TOK_DEV, 2, D)
    gate_view = gates.reshape(N_DP, TOK_DEV, 2)
    layer_out = out_pairs[:, :, 0] * gate_view[:, :, 0:1] + out_pairs[:, :, 1] * gate_view[:, :, 1:2]
    layer_out = layer_out.astype(jnp.bfloat16).reshape(TOKENS, D)
    grad_tokens = (dx_pairs[:, :, 0] + dx_pairs[:, :, 1]).astype(jnp.bfloat16).reshape(TOKENS, D)
    grad_gates = lax.optimization_barrier(jnp.sum(cot_blocks[:, :, None, :] * out_pairs, axis=3)).reshape(TOKENS, 2)
    return (layer_out, grad_tokens, grad_gates, grad_in, grad_out)
```

```python
import jax
import jax.numpy as jnp
from jax import lax
from jax.experimental import pallas as pl
from jax.experimental.pallas import tpu as pltpu
from jax.sharding import PartitionSpec as P


def gelu_tanh(values):
    return jax.nn.gelu(values, approximate=True)


def shards(tokens, routes, gate_values, expert_in, expert_out, cotangent):
    tok_dev, columns = tokens.shape
    groups = lax.axis_size("expert")
    per_dev = expert_in.shape[0]
    experts = per_dev * groups
    capacity = 5 * tok_dev // (2 * experts)
    full_width = columns * groups
    slot_rows = per_dev * capacity
    slot_count = experts * capacity
    flat_routes = routes.reshape(-1)
    onehot = (flat_routes[:, None] == jnp.arange(experts, dtype=jnp.int32)[None, :]).astype(
        jnp.int32
    )
    rank_in = jnp.sum((jnp.cumsum(onehot, axis=0, dtype=jnp.int32) - onehot) * onehot, axis=1)
    owner_idx = flat_routes // per_dev
    within = flat_routes % per_dev
    slot_ids = (within * capacity + rank_in) * groups + owner_idx
    placing = (slot_ids[:, None] == jnp.arange(slot_count, dtype=jnp.int32)[None, :]).astype(
        jnp.bfloat16
    )
    pair_gates = gate_values.reshape(-1)
    pair_tokens = jnp.repeat(tokens, 2, axis=0)
    cot_float = cotangent.astype(jnp.float32)
    pair_cot = (jnp.repeat(cot_float, 2, axis=0) * pair_gates[:, None]).astype(jnp.bfloat16)

    def to_slots(pairs):
        slots = jnp.einsum("ps,pc->sc", placing, pairs, preferred_element_type=jnp.float32)
        return slots.astype(jnp.bfloat16).reshape(slot_rows, groups, columns)

    def from_slots(back):
        return jnp.einsum(
            "ps,sc->pc",
            placing,
            back.reshape(slot_count, columns),
            preferred_element_type=jnp.float32,
        )

    def as_rows(gathered):
        return gathered.reshape(-1, per_dev, capacity, full_width)

    x_moved = lax.all_to_all(
        to_slots(pair_tokens), "expert", split_axis=1, concat_axis=1, tiled=True
    )
    x_rows = as_rows(
        lax.all_gather(x_moved.reshape(slot_rows, full_width), "dp", axis=0, tiled=True)
    )
    pre_act = jnp.einsum("bjcd,jdf->bjcf", x_rows, expert_in, preferred_element_type=jnp.float32)
    pre_act, hidden = (pre_act, gelu_tanh(pre_act).astype(jnp.bfloat16))
    part = hidden
    term = jnp.einsum("bjcf,jfd->bjcd", part, expert_out, preferred_element_type=jnp.float32)
    out_sum = lax.psum_scatter(
        term.reshape(lax.axis_size("dp") * slot_rows, full_width).astype(jnp.bfloat16),
        "dp",
        scatter_dimension=0,
        tiled=True,
    )
    out_back = lax.all_to_all(
        out_sum.reshape(slot_rows, groups, columns),
        "expert",
        split_axis=1,
        concat_axis=1,
        tiled=True,
    )
    dy_moved = lax.all_to_all(to_slots(pair_cot), "expert", split_axis=1, concat_axis=1, tiled=True)
    dy_rows = as_rows(
        lax.all_gather(dy_moved.reshape(slot_rows, full_width), "dp", axis=0, tiled=True)
    )
    d_hidden = jnp.einsum("bjcd,jfd->bjcf", dy_rows, expert_out, preferred_element_type=jnp.float32)
    backward_d_pre = jax.vjp(gelu_tanh, pre_act)[1](d_hidden)[0].astype(jnp.bfloat16)
    grad_out = jnp.einsum("bjcf,bjcd->jfd", hidden, dy_rows, preferred_element_type=jnp.float32)
    grad_in = jnp.einsum(
        "bjcd,bjcf->jdf", x_rows, backward_d_pre, preferred_element_type=jnp.float32
    )
    d_pre, grad_in, grad_out = (
        backward_d_pre,
        grad_in.astype(jnp.bfloat16),
        grad_out.astype(jnp.bfloat16),
    )
    part = d_pre
    term = jnp.einsum("bjcf,jdf->bjcd", part, expert_in, preferred_element_type=jnp.float32)
    dx_sum = lax.psum_scatter(
        term.reshape(lax.axis_size("dp") * slot_rows, full_width).astype(jnp.bfloat16),
        "dp",
        scatter_dimension=0,
        tiled=True,
    )
    dx_back = lax.all_to_all(
        dx_sum.reshape(slot_rows, groups, columns),
        "expert",
        split_axis=1,
        concat_axis=1,
        tiled=True,
    )
    out_view = from_slots(out_back).reshape(tok_dev, 2, columns)
    dx_view = from_slots(dx_back).reshape(tok_dev, 2, columns)
    gate_pairs = pair_gates.reshape(tok_dev, 2)
    layer_out = (out_view[:, 0] * gate_pairs[:, 0:1] + out_view[:, 1] * gate_pairs[:, 1:2]).astype(
        jnp.bfloat16
    )
    grad_tokens = (dx_view[:, 0] + dx_view[:, 1]).astype(jnp.bfloat16)
    gate_part = jnp.sum(cot_float[:, None, :] * out_view, axis=2)
    grad_gates = lax.psum(gate_part, "expert")
    return (layer_out, grad_tokens, grad_gates, grad_in, grad_out)


MESH = pl.DeviceIdType.MESH
BF16 = jnp.bfloat16
F32 = jnp.float32


def tiles_of(width, step=256):
    return [(lo, min(step, width - lo)) for lo in range(0, width, step)]


def dot(left, right, contract):
    return lax.dot_general(left, right, ((contract[:1], contract[1:]), ((), ())), preferred_element_type=F32)


def layer_kernel(
    tok_ref, cot_ref, routes_t, gates_t, gates_ref, w_in_hbm, w_out_hbm,
    out_ref, gtok_ref, gg_ref, gi_hbm, go_hbm,
    w_in, w_out, gi, go, slots, zgot, gath, rows, hid, slope, dpre,
    term, mate, sums, relay, landed, zsend, zback, place, gpart,
    wsem, osem, a2a_s, a2a_r, ag_s, ag_r, mate_s, mate_r, rs_s, rs_r, back_s, back_r, gg_s, gg_r,
):
    tok_dev, cols = tok_ref.shape
    zs = slots.shape[1]
    per_rows = slots.shape[2]
    per_dev = w_in.shape[0]
    cap = per_rows // per_dev
    width, hidden_here = w_in.shape[1:]
    experts = zs * per_dev
    z = lax.axis_index("expert")
    d = lax.axis_index("dp")
    core = d % 2
    xbit = (d // 2) % 2
    ybit = d // 4
    mate_d = d + 1 - 2 * core
    xn = d + 2 - 4 * xbit
    yn = d + 4 - 8 * ybit
    dd = xn + 4 - 8 * ybit
    first = core * yn + (1 - core) * xn
    second = core * xn + (1 - core) * yn

    def remote(src, dst, send, recv, zi, di):
        return pltpu.make_async_remote_copy(
            src_ref=src, dst_ref=dst, send_sem=send, recv_sem=recv, device_id=(zi, di), device_id_type=MESH
        )

    barrier = pltpu.get_barrier_semaphore()
    for step in range(1, zs):
        pl.semaphore_signal(barrier, inc=1, device_id=((z + step) % zs, d), device_id_type=MESH)
    for other in (mate_d, xn, yn):
        pl.semaphore_signal(barrier, inc=1, device_id=(z, other), device_id_type=MESH)

    w_copies = []
    for j in range(per_dev):
        w_copies.append(pltpu.make_async_copy(w_in_hbm.at[j], w_in.at[j], wsem.at[0, j]))
        w_copies.append(pltpu.make_async_copy(w_out_hbm.at[j], w_out.at[j], wsem.at[1, j]))
    for copy in w_copies:
        copy.start()

    named = lax.broadcasted_iota(jnp.int32, (experts, tok_dev), 0)
    first_of = (named == routes_t[0:1, :]).astype(F32)
    second_of = (named == routes_t[1:2, :]).astype(F32)
    before = (
        lax.broadcasted_iota(jnp.int32, (tok_dev, tok_dev), 0)
        < lax.broadcasted_iota(jnp.int32, (tok_dev, tok_dev), 1)
    ).astype(F32).astype(BF16)
    earlier = dot((first_of + second_of).astype(BF16), before, (1, 0))
    slot_iota = lax.broadcasted_iota(jnp.int32, (experts * cap, tok_dev), 0)
    gate_col = jnp.zeros((experts * cap, 1), F32)
    for k, of in ((0, first_of), (1, second_of)):
        rank = jnp.sum(earlier * of, axis=0, keepdims=True).astype(jnp.int32)
        taken = (slot_iota == routes_t[k : k + 1, :] * cap + rank).astype(F32)
        place[k] = taken.astype(BF16)
        gate_col = gate_col + jnp.sum(taken * gates_t[k : k + 1, :], axis=1, keepdims=True)
    both = place[0] + place[1]
    slots[0] = dot(both, tok_ref[...], (1, 0)).astype(BF16).reshape(zs, per_rows, cols)
    slots[1] = (dot(both, cot_ref[...], (1, 0)) * gate_col).astype(BF16).reshape(zs, per_rows, cols)
    for a in range(2):
        zgot[a, pl.ds(z, 1)] = slots[a, pl.ds(z, 1)]

    pl.semaphore_wait(barrier, zs + 2)

    a2a = []
    for a in range(2):
        a2a.append([])
        for step in range(1, zs):
            to = (z + step) % zs
            copy = remote(
                slots.at[a, to], zgot.at[a, z], a2a_s.at[a, step - 1], a2a_r.at[a, step - 1], to, d
            )
            copy.start()
            a2a[a].append(copy)

    def ag_copy(a, i):
        block, to = (
            (d, xn), (d, yn), (d, mate_d),
            (second, first), (xn, mate_d), (yn, mate_d), (dd, mate_d),
        )[i]
        return remote(gath.at[a, block], gath.at[a, block], ag_s.at[a, i], ag_r.at[a, i], z, to)

    ag = [[ag_copy(a, i) for i in range(7)] for a in range(2)]

    def assemble(a):
        for copy in a2a[a]:
            copy.wait()
        whole = jnp.concatenate([zgot[a, i].astype(F32) for i in range(zs)], axis=-1)
        gath[a, pl.ds(d, 1)] = whole.astype(BF16)[None]
        for i in range(3):
            ag[a][i].start()

    def forward(a):
        ag[a][0].wait_recv()
        ag[a][1].wait_recv()
        for i in (3, 4, 5):
            ag[a][i].start()

    def forward_last(a):
        ag[a][3].wait_recv()
        ag[a][6].start()

    def finish(a):
        for i in (2, 4, 5, 6):
            ag[a][i].wait_recv()

        def column(n, carry):
            at = pl.ds(pl.multiple_of(n * 128, 128), 128)
            for half in range(2):
                blocks = [gath[a, 2 * chip + half, :, at].astype(F32) for chip in range(4)]
                for w in range(per_dev):
                    picked = jnp.concatenate([b[w * cap : (w + 1) * cap] for b in blocks], axis=0)
                    rows[a, w, half * 4 * cap : (half + 1) * 4 * cap, at] = picked.astype(BF16)
            return carry

        lax.fori_loop(0, width // 128, column, 0)

    def activation(j):
        def column(n, carry):
            at = pl.ds(pl.multiple_of(n * 256, 256), 256)
            v = dot(rows[0, j], w_in[j, :, at], (1, 0))
            scale = 0.7978845608028654
            sq = v * v
            t = jnp.tanh(scale * v * (1.0 + 0.044715 * sq))
            half = 0.5 * (1.0 + t)
            hid[j, :, at] = (v * half).astype(BF16)
            slope[j, :, at] = half + 0.5 * v * (1.0 - t * t) * (scale * (1.0 + 0.134145 * sq))
            return carry

        lax.fori_loop(0, hidden_here // 256, column, 0)

    def backward(j):
        def column(n, carry):
            at = pl.ds(pl.multiple_of(n * 256, 256), 256)
            dh = dot(rows[1, j], w_out[j, at, :], (1, 1))
            dpre[j, :, at] = (slope[j, :, at] * dh).astype(BF16)
            return carry

        lax.fori_loop(0, hidden_here // 256, column, 0)

    half_rows = 4 * cap

    def mate_copy(a, j):
        return remote(
            term.at[a, j, 1 - core], mate.at[a, j], mate_s.at[a, j], mate_r.at[a, j], z, mate_d
        )

    mates = [[mate_copy(a, j) for j in range(per_dev)] for a in range(2)]

    def terms(a, j):
        for lo, size in tiles_of(width):
            if a == 0:
                v = dot(hid[j], w_out[j, :, lo : lo + size], (1, 0))
            else:
                v = dot(dpre[j], w_in[j, lo : lo + size, :], (1, 1))
            term[a, j, :, :, lo : lo + size] = v.astype(BF16).reshape(2, half_rows, size)
        mates[a][j].start()

    def rs_copy(a, i):
        src, to = ((sums.at[a, dd // 2], first), (sums.at[a, first // 2], first), (relay.at[a], second))[i]
        return remote(src, landed.at[a, i], rs_s.at[a, i], rs_r.at[a, i], z, to)

    rs = [[rs_copy(a, i) for i in range(3)] for a in range(2)]

    def rs_start(a):
        for j in range(per_dev):
            mates[a][j].wait()

        def column(n, carry):
            at = pl.ds(pl.multiple_of(n * 128, 128), 128)
            parts = [
                term[a, j, core, :, at].astype(F32) + mate[a, j, :, at].astype(F32)
                for j in range(per_dev)
            ]
            for chip in range(4):
                picked = jnp.concatenate([p[chip * cap : (chip + 1) * cap] for p in parts], axis=0)
                sums[a, chip, :, at] = picked.astype(BF16)
            return carry

        lax.fori_loop(0, width // 128, column, 0)
        rs[a][0].start()
        rs[a][1].start()

    def rs_relay(a):
        rs[a][0].wait()
        relay[a] = (sums[a, second // 2].astype(F32) + landed[a, 0].astype(F32)).astype(BF16)
        rs[a][2].start()

    def back_copy(a, step):
        to = (z + step) % zs
        return remote(
            zsend.at[a, to], zback.at[a, z], back_s.at[a, step - 1], back_r.at[a, step - 1], to, d
        )

    back = [[back_copy(a, step) for step in range(1, zs)] for a in range(2)]

    def rs_end(a):
        rs[a][1].wait()
        rs[a][2].wait()
        total = sums[a, d // 2].astype(F32) + landed[a, 1].astype(F32) + landed[a, 2].astype(F32)
        for i in range(zs):
            zsend[a, i] = total[:, i * cols : (i + 1) * cols].astype(BF16)
        zback[a, pl.ds(z, 1)] = zsend[a, pl.ds(z, 1)]
        for copy in back[a]:
            copy.start()

    def weight_grad_out(j):
        def part(m, carry):
            at = pl.ds(pl.multiple_of(m * 256, 256), 256)
            left = hid[j, :, at]
            for lo, size in tiles_of(width):
                go[j, at, lo : lo + size] = dot(left, rows[1, j, :, lo : lo + size], (0, 0)).astype(BF16)
            return carry

        lax.fori_loop(0, hidden_here // 256, part, 0)
        copy = pltpu.make_async_copy(go.at[j], go_hbm.at[j], osem.at[0, j])
        copy.start()
        return copy

    def weight_grad_in(j):
        def part(m, carry):
            at = pl.ds(pl.multiple_of(m * 128, 128), 128)
            gi[j, at, :] = dot(rows[0, j, :, at], dpre[j], (0, 0)).astype(BF16)
            return carry

        lax.fori_loop(0, width // 128, part, 0)
        copy = pltpu.make_async_copy(gi.at[j], gi_hbm.at[j], osem.at[1, j])
        copy.start()
        return copy

    gg = []
    for step in range(1, zs):
        gg.append(
            remote(
                gpart.at[z], gpart.at[z], gg_s.at[step - 1], gg_r.at[step - 1], (z + step) % zs, d
            )
        )

    def combine(a):
        for copy in back[a]:
            copy.wait()
        slot_rows = zback[a].reshape(zs * per_rows, cols)
        views = [dot(place[k], slot_rows, (0, 0)) for k in range(2)]
        if a == 1:
            gtok_ref[...] = (views[0] + views[1]).astype(BF16)
            return
        out_ref[...] = (views[0] * gates_ref[:, 0:1] + views[1] * gates_ref[:, 1:2]).astype(BF16)
        cot = cot_ref[...].astype(F32)
        inner = [jnp.sum(cot * v, axis=1, keepdims=True) for v in views]
        lane = lax.broadcasted_iota(jnp.int32, (tok_dev, 128), 1)
        gpart[pl.ds(z, 1)] = jnp.where(lane == 0, inner[0], inner[1])[None]
        for copy in gg:
            copy.start()

    assemble(0)
    assemble(1)
    forward(0)
    forward_last(0)
    for copy in w_copies:
        copy.wait()
    finish(0)
    activation(0)
    forward(1)
    activation(1)
    forward_last(1)
    terms(0, 0)
    terms(0, 1)
    finish(1)
    backward(0)
    rs_start(0)
    terms(1, 0)
    backward(1)
    rs_relay(0)
    terms(1, 1)
    rs_end(0)
    outs = [weight_grad_out(0)]
    rs_start(1)
    outs.append(weight_grad_out(1))
    rs_relay(1)
    outs.append(weight_grad_in(0))
    combine(0)
    rs_end(1)
    outs.append(weight_grad_in(1))
    for copy in gg:
        copy.wait()
    total = gpart[0] + gpart[1] + gpart[2] + gpart[3]
    gg_ref[...] = total[:, 0:2]
    combine(1)
    for a in range(2):
        for copy in ag[a]:
            copy.wait_send()
    for copy in outs:
        copy.wait()


def fused_shards(tokens, routes, gate_values, expert_in, expert_out, cotangent):
    tok_dev, cols = tokens.shape
    zs = lax.axis_size("expert")
    dps = lax.axis_size("dp")
    per_dev, width, hidden_here = expert_in.shape
    experts = per_dev * zs
    cap = 5 * tok_dev // (2 * experts)
    per_rows = per_dev * cap
    all_rows = dps * cap
    vmem = pl.BlockSpec(memory_space=pltpu.VMEM)
    hbm = pl.BlockSpec(memory_space=pl.ANY)
    dma = pltpu.SemaphoreType.DMA
    return pl.pallas_call(
        layer_kernel,
        out_shape=(
            jax.ShapeDtypeStruct(tokens.shape, BF16),
            jax.ShapeDtypeStruct(tokens.shape, BF16),
            jax.ShapeDtypeStruct(gate_values.shape, F32),
            jax.ShapeDtypeStruct(expert_in.shape, BF16),
            jax.ShapeDtypeStruct(expert_out.shape, BF16),
        ),
        in_specs=[vmem] * 5 + [hbm] * 2,
        out_specs=(vmem, vmem, vmem, hbm, hbm),
        scratch_shapes=[
            pltpu.VMEM(expert_in.shape, BF16),
            pltpu.VMEM(expert_out.shape, BF16),
            pltpu.VMEM(expert_in.shape, BF16),
            pltpu.VMEM(expert_out.shape, BF16),
            pltpu.VMEM((2, zs, per_rows, cols), BF16),
            pltpu.VMEM((2, zs, per_rows, cols), BF16),
            pltpu.VMEM((2, dps, per_rows, width), BF16),
            pltpu.VMEM((2, per_dev, all_rows, width), BF16),
            pltpu.VMEM((per_dev, all_rows, hidden_here), BF16),
            pltpu.VMEM((per_dev, all_rows, hidden_here), F32),
            pltpu.VMEM((per_dev, all_rows, hidden_here), BF16),
            pltpu.VMEM((2, per_dev, 2, all_rows // 2, width), BF16),
            pltpu.VMEM((2, per_dev, all_rows // 2, width), BF16),
            pltpu.VMEM((2, dps // 2, per_rows, width), BF16),
            pltpu.VMEM((2, per_rows, width), BF16),
            pltpu.VMEM((2, 3, per_rows, width), BF16),
            pltpu.VMEM((2, zs, per_rows, cols), BF16),
            pltpu.VMEM((2, zs, per_rows, cols), BF16),
            pltpu.VMEM((2, experts * cap, tok_dev), BF16),
            pltpu.VMEM((zs, tok_dev, 128), F32),
            dma((2, per_dev)), dma((2, per_dev)),
            dma((2, zs - 1)), dma((2, zs - 1)),
            dma((2, 7)), dma((2, 7)),
            dma((2, per_dev)), dma((2, per_dev)),
            dma((2, 3)), dma((2, 3)),
            dma((2, zs - 1)), dma((2, zs - 1)),
            dma((zs - 1,)), dma((zs - 1,)),
        ],
        compiler_params=pltpu.CompilerParams(
            collective_id=0, has_side_effects=True, vmem_limit_bytes=62 * 1024 * 1024
        ),
    )(tokens, cotangent, routes.T, gate_values.T, gate_values, expert_in, expert_out)


def solution(mesh):
    placed = (
        P("dp", "expert"),
        P("dp", None),
        P("dp", None),
        P("expert", None, "dp"),
        P("expert", "dp", None),
        P("dp", "expert"),
    )
    fused = mesh.shape["expert"] == 4 and mesh.shape["dp"] == 8
    return jax.shard_map(
        fused_shards if fused else shards,
        mesh=mesh,
        in_specs=placed,
        out_specs=(
            P("dp", "expert"),
            P("dp", "expert"),
            P("dp", None),
            P("expert", None, "dp"),
            P("expert", "dp", None),
        ),
        check_vma=False,
    )
```

```python
import jax
import jax.numpy as jnp
from jax import lax
from jax.experimental import pallas as pl
from jax.experimental.pallas import tpu as pltpu
from jax.sharding import PartitionSpec as P


def gelu_tanh(values):
    return jax.nn.gelu(values, approximate=True)


def shards(tokens, routes, gate_values, expert_in, expert_out, cotangent):
    tok_dev, columns = tokens.shape
    groups = lax.axis_size("expert")
    per_dev = expert_in.shape[0]
    experts = per_dev * groups
    capacity = 5 * tok_dev // (2 * experts)
    full_width = columns * groups
    slot_rows = per_dev * capacity
    slot_count = experts * capacity
    flat_routes = routes.reshape(-1)
    onehot = (flat_routes[:, None] == jnp.arange(experts, dtype=jnp.int32)[None, :]).astype(
        jnp.int32
    )
    rank_in = jnp.sum((jnp.cumsum(onehot, axis=0, dtype=jnp.int32) - onehot) * onehot, axis=1)
    owner_idx = flat_routes // per_dev
    within = flat_routes % per_dev
    slot_ids = (within * capacity + rank_in) * groups + owner_idx
    placing = (slot_ids[:, None] == jnp.arange(slot_count, dtype=jnp.int32)[None, :]).astype(
        jnp.bfloat16
    )
    pair_gates = gate_values.reshape(-1)
    pair_tokens = jnp.repeat(tokens, 2, axis=0)
    cot_float = cotangent.astype(jnp.float32)
    pair_cot = (jnp.repeat(cot_float, 2, axis=0) * pair_gates[:, None]).astype(jnp.bfloat16)

    def to_slots(pairs):
        slots = jnp.einsum("ps,pc->sc", placing, pairs, preferred_element_type=jnp.float32)
        return slots.astype(jnp.bfloat16).reshape(slot_rows, groups, columns)

    def from_slots(back):
        return jnp.einsum(
            "ps,sc->pc",
            placing,
            back.reshape(slot_count, columns),
            preferred_element_type=jnp.float32,
        )

    def as_rows(gathered):
        return gathered.reshape(-1, per_dev, capacity, full_width)

    x_moved = lax.all_to_all(
        to_slots(pair_tokens), "expert", split_axis=1, concat_axis=1, tiled=True
    )
    x_rows = as_rows(
        lax.all_gather(x_moved.reshape(slot_rows, full_width), "dp", axis=0, tiled=True)
    )
    pre_act = jnp.einsum("bjcd,jdf->bjcf", x_rows, expert_in, preferred_element_type=jnp.float32)
    pre_act, hidden = (pre_act, gelu_tanh(pre_act).astype(jnp.bfloat16))
    part = hidden
    term = jnp.einsum("bjcf,jfd->bjcd", part, expert_out, preferred_element_type=jnp.float32)
    out_sum = lax.psum_scatter(
        term.reshape(lax.axis_size("dp") * slot_rows, full_width).astype(jnp.bfloat16),
        "dp",
        scatter_dimension=0,
        tiled=True,
    )
    out_back = lax.all_to_all(
        out_sum.reshape(slot_rows, groups, columns),
        "expert",
        split_axis=1,
        concat_axis=1,
        tiled=True,
    )
    dy_moved = lax.all_to_all(to_slots(pair_cot), "expert", split_axis=1, concat_axis=1, tiled=True)
    dy_rows = as_rows(
        lax.all_gather(dy_moved.reshape(slot_rows, full_width), "dp", axis=0, tiled=True)
    )
    d_hidden = jnp.einsum("bjcd,jfd->bjcf", dy_rows, expert_out, preferred_element_type=jnp.float32)
    backward_d_pre = jax.vjp(gelu_tanh, pre_act)[1](d_hidden)[0].astype(jnp.bfloat16)
    grad_out = jnp.einsum("bjcf,bjcd->jfd", hidden, dy_rows, preferred_element_type=jnp.float32)
    grad_in = jnp.einsum(
        "bjcd,bjcf->jdf", x_rows, backward_d_pre, preferred_element_type=jnp.float32
    )
    d_pre, grad_in, grad_out = (
        backward_d_pre,
        grad_in.astype(jnp.bfloat16),
        grad_out.astype(jnp.bfloat16),
    )
    part = d_pre
    term = jnp.einsum("bjcf,jdf->bjcd", part, expert_in, preferred_element_type=jnp.float32)
    dx_sum = lax.psum_scatter(
        term.reshape(lax.axis_size("dp") * slot_rows, full_width).astype(jnp.bfloat16),
        "dp",
        scatter_dimension=0,
        tiled=True,
    )
    dx_back = lax.all_to_all(
        dx_sum.reshape(slot_rows, groups, columns),
        "expert",
        split_axis=1,
        concat_axis=1,
        tiled=True,
    )
    out_view = from_slots(out_back).reshape(tok_dev, 2, columns)
    dx_view = from_slots(dx_back).reshape(tok_dev, 2, columns)
    gate_pairs = pair_gates.reshape(tok_dev, 2)
    layer_out = (out_view[:, 0] * gate_pairs[:, 0:1] + out_view[:, 1] * gate_pairs[:, 1:2]).astype(
        jnp.bfloat16
    )
    grad_tokens = (dx_view[:, 0] + dx_view[:, 1]).astype(jnp.bfloat16)
    gate_part = jnp.sum(cot_float[:, None, :] * out_view, axis=2)
    grad_gates = lax.psum(gate_part, "expert")
    return (layer_out, grad_tokens, grad_gates, grad_in, grad_out)


MESH = pl.DeviceIdType.MESH
BF16 = jnp.bfloat16
F32 = jnp.float32


def tiles_of(width, step=256):
    return [(lo, min(step, width - lo)) for lo in range(0, width, step)]


def dot(left, right, contract):
    return lax.dot_general(left, right, ((contract[:1], contract[1:]), ((), ())), preferred_element_type=F32)


def layer_kernel(
    tok_ref, cot_ref, routes_t, gates_t, w_in_hbm, w_out_hbm,
    out_ref, gtok_ref, gg_ref, gi, go,
    w_in, w_out, slots, zgot, gath, rows, hid, slope, dpre,
    term, mate, sums, relay, landed, zsend, zback, place, gpart,
    wsem, a2a_s, a2a_r, ag_s, ag_r, mate_s, mate_r, rs_s, rs_r, back_s, back_r, gg_s, gg_r,
):
    cols, tok_dev = tok_ref.shape
    zs = slots.shape[1]
    per_rows = slots.shape[2]
    per_dev = w_in.shape[0]
    cap = per_rows // per_dev
    width, hidden_here = w_in.shape[1:]
    experts = zs * per_dev
    z = lax.axis_index("expert")
    d = lax.axis_index("dp")
    core = d % 2
    xbit = (d // 2) % 2
    ybit = d // 4
    mate_d = d + 1 - 2 * core
    xn = d + 2 - 4 * xbit
    yn = d + 4 - 8 * ybit
    dd = xn + 4 - 8 * ybit
    first = core * yn + (1 - core) * xn
    second = core * xn + (1 - core) * yn

    def remote(src, dst, send, recv, zi, di):
        return pltpu.make_async_remote_copy(
            src_ref=src, dst_ref=dst, send_sem=send, recv_sem=recv, device_id=(zi, di), device_id_type=MESH
        )

    barrier = pltpu.get_barrier_semaphore()
    for step in range(1, zs):
        pl.semaphore_signal(barrier, inc=1, device_id=((z + step) % zs, d), device_id_type=MESH)
    for other in (mate_d, xn, yn):
        pl.semaphore_signal(barrier, inc=1, device_id=(z, other), device_id_type=MESH)

    w_copies = []
    for j in range(per_dev):
        w_copies.append(pltpu.make_async_copy(w_in_hbm.at[j], w_in.at[j], wsem.at[0, j]))
        w_copies.append(pltpu.make_async_copy(w_out_hbm.at[j], w_out.at[j], wsem.at[1, j]))
    for copy in w_copies:
        copy.start()

    named = lax.broadcasted_iota(jnp.int32, (experts, tok_dev), 0)
    first_of = (named == routes_t[0:1, :]).astype(F32)
    second_of = (named == routes_t[1:2, :]).astype(F32)
    before = (
        lax.broadcasted_iota(jnp.int32, (tok_dev, tok_dev), 0)
        < lax.broadcasted_iota(jnp.int32, (tok_dev, tok_dev), 1)
    ).astype(F32).astype(BF16)
    earlier = dot((first_of + second_of).astype(BF16), before, (1, 0))
    slot_iota = lax.broadcasted_iota(jnp.int32, (experts * cap, tok_dev), 0)
    gate_col = jnp.zeros((experts * cap, 1), F32)
    for k, of in ((0, first_of), (1, second_of)):
        rank = jnp.sum(earlier * of, axis=0, keepdims=True).astype(jnp.int32)
        taken = (slot_iota == routes_t[k : k + 1, :] * cap + rank).astype(F32)
        place[k] = taken.astype(BF16)
        gate_col = gate_col + jnp.sum(taken * gates_t[k : k + 1, :], axis=1, keepdims=True)
    both = place[0] + place[1]
    slots[0] = dot(both, tok_ref[...], (1, 1)).astype(BF16).reshape(zs, per_rows, cols)
    slots[1] = (dot(both, cot_ref[...], (1, 1)) * gate_col).astype(BF16).reshape(zs, per_rows, cols)
    for a in range(2):
        zgot[a, pl.ds(z, 1)] = slots[a, pl.ds(z, 1)]

    pl.semaphore_wait(barrier, zs + 2)

    a2a = []
    for a in range(2):
        a2a.append([])
        for step in range(1, zs):
            to = (z + step) % zs
            copy = remote(
                slots.at[a, to], zgot.at[a, z], a2a_s.at[a, step - 1], a2a_r.at[a, step - 1], to, d
            )
            copy.start()
            a2a[a].append(copy)

    def ag_copy(a, i):
        block, to = (
            (d, xn), (d, yn), (d, mate_d),
            (second, first), (xn, mate_d), (yn, mate_d), (dd, mate_d),
        )[i]
        return remote(gath.at[a, block], gath.at[a, block], ag_s.at[a, i], ag_r.at[a, i], z, to)

    ag = [[ag_copy(a, i) for i in range(7)] for a in range(2)]

    def assemble(a):
        for copy in a2a[a]:
            copy.wait()
        whole = jnp.concatenate([zgot[a, i].astype(F32) for i in range(zs)], axis=-1)
        gath[a, pl.ds(d, 1)] = whole.astype(BF16)[None]
        for i in range(3):
            ag[a][i].start()

    def forward(a):
        ag[a][0].wait_recv()
        ag[a][1].wait_recv()
        for i in (3, 4, 5):
            ag[a][i].start()

    def forward_last(a):
        ag[a][3].wait_recv()
        ag[a][6].start()

    def finish(a):
        for i in (2, 4, 5, 6):
            ag[a][i].wait_recv()

        def column(n, carry):
            at = pl.ds(pl.multiple_of(n * 128, 128), 128)
            for half in range(2):
                blocks = [gath[a, 2 * chip + half, :, at].astype(F32) for chip in range(4)]
                for w in range(per_dev):
                    picked = jnp.concatenate([b[w * cap : (w + 1) * cap] for b in blocks], axis=0)
                    rows[a, w, half * 4 * cap : (half + 1) * 4 * cap, at] = picked.astype(BF16)
            return carry

        lax.fori_loop(0, width // 128, column, 0)

    def activation(j):
        def column(n, carry):
            at = pl.ds(pl.multiple_of(n * 256, 256), 256)
            v = dot(rows[0, j], w_in[j, :, at], (1, 0))
            scale = 0.7978845608028654
            sq = v * v
            t = jnp.tanh(scale * v * (1.0 + 0.044715 * sq))
            half = 0.5 * (1.0 + t)
            hid[j, :, at] = (v * half).astype(BF16)
            slope[j, :, at] = half + 0.5 * v * (1.0 - t * t) * (scale * (1.0 + 0.134145 * sq))
            return carry

        lax.fori_loop(0, hidden_here // 256, column, 0)

    def backward(j):
        def column(n, carry):
            at = pl.ds(pl.multiple_of(n * 256, 256), 256)
            dh = dot(rows[1, j], w_out[j, at, :], (1, 1))
            dpre[j, :, at] = (slope[j, :, at] * dh).astype(BF16)
            return carry

        lax.fori_loop(0, hidden_here // 256, column, 0)

    half_rows = 4 * cap

    def mate_copy(a, j):
        return remote(
            term.at[a, j, 1 - core], mate.at[a, j], mate_s.at[a, j], mate_r.at[a, j], z, mate_d
        )

    mates = [[mate_copy(a, j) for j in range(per_dev)] for a in range(2)]

    def terms(a, j):
        for lo, size in tiles_of(width):
            if a == 0:
                v = dot(hid[j], w_out[j, :, lo : lo + size], (1, 0))
            else:
                v = dot(dpre[j], w_in[j, lo : lo + size, :], (1, 1))
            term[a, j, :, :, lo : lo + size] = v.astype(BF16).reshape(2, half_rows, size)
        mates[a][j].start()

    def rs_copy(a, i):
        src, to = ((sums.at[a, dd // 2], first), (sums.at[a, first // 2], first), (relay.at[a], second))[i]
        return remote(src, landed.at[a, i], rs_s.at[a, i], rs_r.at[a, i], z, to)

    rs = [[rs_copy(a, i) for i in range(3)] for a in range(2)]

    def rs_start(a):
        for j in range(per_dev):
            mates[a][j].wait()

        def column(n, carry):
            at = pl.ds(pl.multiple_of(n * 128, 128), 128)
            parts = [
                term[a, j, core, :, at].astype(F32) + mate[a, j, :, at].astype(F32)
                for j in range(per_dev)
            ]
            for chip in range(4):
                picked = jnp.concatenate([p[chip * cap : (chip + 1) * cap] for p in parts], axis=0)
                sums[a, chip, :, at] = picked.astype(BF16)
            return carry

        lax.fori_loop(0, width // 128, column, 0)
        rs[a][0].start()
        rs[a][1].start()

    def rs_relay(a):
        rs[a][0].wait()
        relay[a] = (sums[a, second // 2].astype(F32) + landed[a, 0].astype(F32)).astype(BF16)
        rs[a][2].start()

    def back_copy(a, step):
        to = (z + step) % zs
        return remote(
            zsend.at[a, to], zback.at[a, z], back_s.at[a, step - 1], back_r.at[a, step - 1], to, d
        )

    back = [[back_copy(a, step) for step in range(1, zs)] for a in range(2)]

    def rs_end(a):
        rs[a][1].wait()
        rs[a][2].wait()
        total = sums[a, d // 2].astype(F32) + landed[a, 1].astype(F32) + landed[a, 2].astype(F32)
        for i in range(zs):
            zsend[a, i] = total[:, i * cols : (i + 1) * cols].astype(BF16)
        zback[a, pl.ds(z, 1)] = zsend[a, pl.ds(z, 1)]
        for copy in back[a]:
            copy.start()

    def weight_grad_out(j):
        def part(m, carry):
            at = pl.ds(pl.multiple_of(m * 256, 256), 256)
            left = hid[j, :, at]
            for lo, size in tiles_of(width):
                go[j, at, lo : lo + size] = dot(left, rows[1, j, :, lo : lo + size], (0, 0)).astype(BF16)
            return carry

        lax.fori_loop(0, hidden_here // 256, part, 0)

    def weight_grad_in(j):
        def part(m, carry):
            at = pl.ds(pl.multiple_of(m * 128, 128), 128)
            gi[j, at, :] = dot(rows[0, j, :, at], dpre[j], (0, 0)).astype(BF16)
            return carry

        lax.fori_loop(0, width // 128, part, 0)

    gg = []
    for step in range(1, zs):
        gg.append(
            remote(
                gpart.at[z], gpart.at[z], gg_s.at[step - 1], gg_r.at[step - 1], (z + step) % zs, d
            )
        )

    def combine(a):
        for copy in back[a]:
            copy.wait()
        slot_rows = zback[a].reshape(zs * per_rows, cols)
        views = [dot(slot_rows, place[k], (0, 0)) for k in range(2)]
        if a == 1:
            gtok_ref[...] = (views[0] + views[1]).astype(BF16)
            return
        out_ref[...] = (views[0] * gates_t[0:1, :] + views[1] * gates_t[1:2, :]).astype(BF16)
        cot = cot_ref[...].astype(F32)
        inner = [jnp.sum(cot * v, axis=0, keepdims=True) for v in views]
        row = lax.broadcasted_iota(jnp.int32, (8, tok_dev), 0)
        gpart[pl.ds(z, 1)] = jnp.where(row == 0, inner[0], inner[1])[None]
        for copy in gg:
            copy.start()

    assemble(0)
    assemble(1)
    forward(0)
    forward_last(0)
    for copy in w_copies:
        copy.wait()
    finish(0)
    activation(0)
    forward(1)
    activation(1)
    forward_last(1)
    terms(0, 0)
    terms(0, 1)
    finish(1)
    backward(0)
    rs_start(0)
    terms(1, 0)
    backward(1)
    rs_relay(0)
    terms(1, 1)
    rs_end(0)
    weight_grad_out(0)
    rs_start(1)
    weight_grad_out(1)
    rs_relay(1)
    weight_grad_in(0)
    combine(0)
    rs_end(1)
    weight_grad_in(1)
    for copy in gg:
        copy.wait()
    total = gpart[0] + gpart[1] + gpart[2] + gpart[3]
    gg_ref[...] = total[0:2]
    combine(1)
    for a in range(2):
        for copy in ag[a]:
            copy.wait_send()


def fused_shards(tokens, routes, gate_values, expert_in, expert_out, cotangent):
    tok_dev, cols = tokens.shape
    zs = lax.axis_size("expert")
    dps = lax.axis_size("dp")
    per_dev, width, hidden_here = expert_in.shape
    experts = per_dev * zs
    cap = 5 * tok_dev // (2 * experts)
    per_rows = per_dev * cap
    all_rows = dps * cap
    vmem = pl.BlockSpec(memory_space=pltpu.VMEM)
    hbm = pl.BlockSpec(memory_space=pl.ANY)
    dma = pltpu.SemaphoreType.DMA
    layer_t, gtok_t, gates_grad_t, grad_in, grad_out = pl.pallas_call(
        layer_kernel,
        out_shape=(
            pltpu.VMEM((cols, tok_dev), BF16),
            pltpu.VMEM((cols, tok_dev), BF16),
            pltpu.VMEM((2, tok_dev), F32),
            pltpu.VMEM(expert_in.shape, BF16),
            pltpu.VMEM(expert_out.shape, BF16),
        ),
        in_specs=[vmem] * 4 + [hbm] * 2,
        out_specs=(vmem,) * 5,
        scratch_shapes=[
            pltpu.VMEM(expert_in.shape, BF16),
            pltpu.VMEM(expert_out.shape, BF16),
            pltpu.VMEM((2, zs, per_rows, cols), BF16),
            pltpu.VMEM((2, zs, per_rows, cols), BF16),
            pltpu.VMEM((2, dps, per_rows, width), BF16),
            pltpu.VMEM((2, per_dev, all_rows, width), BF16),
            pltpu.VMEM((per_dev, all_rows, hidden_here), BF16),
            pltpu.VMEM((per_dev, all_rows, hidden_here), F32),
            pltpu.VMEM((per_dev, all_rows, hidden_here), BF16),
            pltpu.VMEM((2, per_dev, 2, all_rows // 2, width), BF16),
            pltpu.VMEM((2, per_dev, all_rows // 2, width), BF16),
            pltpu.VMEM((2, dps // 2, per_rows, width), BF16),
            pltpu.VMEM((2, per_rows, width), BF16),
            pltpu.VMEM((2, 3, per_rows, width), BF16),
            pltpu.VMEM((2, zs, per_rows, cols), BF16),
            pltpu.VMEM((2, zs, per_rows, cols), BF16),
            pltpu.VMEM((2, experts * cap, tok_dev), BF16),
            pltpu.VMEM((zs, 8, tok_dev), F32),
            dma((2, per_dev)),
            dma((2, zs - 1)), dma((2, zs - 1)),
            dma((2, 7)), dma((2, 7)),
            dma((2, per_dev)), dma((2, per_dev)),
            dma((2, 3)), dma((2, 3)),
            dma((2, zs - 1)), dma((2, zs - 1)),
            dma((zs - 1,)), dma((zs - 1,)),
        ],
        compiler_params=pltpu.CompilerParams(
            collective_id=0, has_side_effects=True, vmem_limit_bytes=46 * 1024 * 1024
        ),
    )(tokens.T, cotangent.T, routes.T, gate_values.T, expert_in, expert_out)
    return (layer_t.T, gtok_t.T, gates_grad_t.T, grad_in, grad_out)


def solution(mesh):
    placed = (
        P("dp", "expert"),
        P("dp", None),
        P("dp", None),
        P("expert", None, "dp"),
        P("expert", "dp", None),
        P("dp", "expert"),
    )
    fused = mesh.shape["expert"] == 4 and mesh.shape["dp"] == 8
    return jax.shard_map(
        fused_shards if fused else shards,
        mesh=mesh,
        in_specs=placed,
        out_specs=(
            P("dp", "expert"),
            P("dp", "expert"),
            P("dp", None),
            P("expert", None, "dp"),
            P("expert", "dp", None),
        ),
        check_vma=False,
    )
```

```python
import jax
import jax.numpy as jnp
from jax import lax
from jax.experimental import pallas as pl
from jax.experimental.pallas import tpu as pltpu
from jax.sharding import PartitionSpec as P


def gelu_tanh(values):
    return jax.nn.gelu(values, approximate=True)


def shards(tokens, routes, gate_values, expert_in, expert_out, cotangent):
    tok_dev, columns = tokens.shape
    groups = lax.axis_size("expert")
    per_dev = expert_in.shape[0]
    experts = per_dev * groups
    capacity = 5 * tok_dev // (2 * experts)
    full_width = columns * groups
    slot_rows = per_dev * capacity
    slot_count = experts * capacity
    flat_routes = routes.reshape(-1)
    onehot = (flat_routes[:, None] == jnp.arange(experts, dtype=jnp.int32)[None, :]).astype(
        jnp.int32
    )
    rank_in = jnp.sum((jnp.cumsum(onehot, axis=0, dtype=jnp.int32) - onehot) * onehot, axis=1)
    owner_idx = flat_routes // per_dev
    within = flat_routes % per_dev
    slot_ids = (within * capacity + rank_in) * groups + owner_idx
    placing = (slot_ids[:, None] == jnp.arange(slot_count, dtype=jnp.int32)[None, :]).astype(
        jnp.bfloat16
    )
    pair_gates = gate_values.reshape(-1)
    pair_tokens = jnp.repeat(tokens, 2, axis=0)
    cot_float = cotangent.astype(jnp.float32)
    pair_cot = (jnp.repeat(cot_float, 2, axis=0) * pair_gates[:, None]).astype(jnp.bfloat16)

    def to_slots(pairs):
        slots = jnp.einsum("ps,pc->sc", placing, pairs, preferred_element_type=jnp.float32)
        return slots.astype(jnp.bfloat16).reshape(slot_rows, groups, columns)

    def from_slots(back):
        return jnp.einsum(
            "ps,sc->pc",
            placing,
            back.reshape(slot_count, columns),
            preferred_element_type=jnp.float32,
        )

    def as_rows(gathered):
        return gathered.reshape(-1, per_dev, capacity, full_width)

    x_moved = lax.all_to_all(
        to_slots(pair_tokens), "expert", split_axis=1, concat_axis=1, tiled=True
    )
    x_rows = as_rows(
        lax.all_gather(x_moved.reshape(slot_rows, full_width), "dp", axis=0, tiled=True)
    )
    pre_act = jnp.einsum("bjcd,jdf->bjcf", x_rows, expert_in, preferred_element_type=jnp.float32)
    pre_act, hidden = (pre_act, gelu_tanh(pre_act).astype(jnp.bfloat16))
    part = hidden
    term = jnp.einsum("bjcf,jfd->bjcd", part, expert_out, preferred_element_type=jnp.float32)
    out_sum = lax.psum_scatter(
        term.reshape(lax.axis_size("dp") * slot_rows, full_width).astype(jnp.bfloat16),
        "dp",
        scatter_dimension=0,
        tiled=True,
    )
    out_back = lax.all_to_all(
        out_sum.reshape(slot_rows, groups, columns),
        "expert",
        split_axis=1,
        concat_axis=1,
        tiled=True,
    )
    dy_moved = lax.all_to_all(to_slots(pair_cot), "expert", split_axis=1, concat_axis=1, tiled=True)
    dy_rows = as_rows(
        lax.all_gather(dy_moved.reshape(slot_rows, full_width), "dp", axis=0, tiled=True)
    )
    d_hidden = jnp.einsum("bjcd,jfd->bjcf", dy_rows, expert_out, preferred_element_type=jnp.float32)
    backward_d_pre = jax.vjp(gelu_tanh, pre_act)[1](d_hidden)[0].astype(jnp.bfloat16)
    grad_out = jnp.einsum("bjcf,bjcd->jfd", hidden, dy_rows, preferred_element_type=jnp.float32)
    grad_in = jnp.einsum(
        "bjcd,bjcf->jdf", x_rows, backward_d_pre, preferred_element_type=jnp.float32
    )
    d_pre, grad_in, grad_out = (
        backward_d_pre,
        grad_in.astype(jnp.bfloat16),
        grad_out.astype(jnp.bfloat16),
    )
    part = d_pre
    term = jnp.einsum("bjcf,jdf->bjcd", part, expert_in, preferred_element_type=jnp.float32)
    dx_sum = lax.psum_scatter(
        term.reshape(lax.axis_size("dp") * slot_rows, full_width).astype(jnp.bfloat16),
        "dp",
        scatter_dimension=0,
        tiled=True,
    )
    dx_back = lax.all_to_all(
        dx_sum.reshape(slot_rows, groups, columns),
        "expert",
        split_axis=1,
        concat_axis=1,
        tiled=True,
    )
    out_view = from_slots(out_back).reshape(tok_dev, 2, columns)
    dx_view = from_slots(dx_back).reshape(tok_dev, 2, columns)
    gate_pairs = pair_gates.reshape(tok_dev, 2)
    layer_out = (out_view[:, 0] * gate_pairs[:, 0:1] + out_view[:, 1] * gate_pairs[:, 1:2]).astype(
        jnp.bfloat16
    )
    grad_tokens = (dx_view[:, 0] + dx_view[:, 1]).astype(jnp.bfloat16)
    gate_part = jnp.sum(cot_float[:, None, :] * out_view, axis=2)
    grad_gates = lax.psum(gate_part, "expert")
    return (layer_out, grad_tokens, grad_gates, grad_in, grad_out)


MESH = pl.DeviceIdType.MESH
BF16 = jnp.bfloat16
F32 = jnp.float32


def tiles_of(width, step=256):
    return [(lo, min(step, width - lo)) for lo in range(0, width, step)]


def dot(left, right, contract):
    return lax.dot_general(left, right, ((contract[:1], contract[1:]), ((), ())), preferred_element_type=F32)


def layer_kernel(
    tok_ref, cot_ref, routes_t, gates_t, w_in_hbm, w_out_hbm,
    out_ref, gtok_ref, gg_ref, gi, go,
    w_in, w_out, slots, zgot, gath, rows, hid, slope, dpre,
    term, mate, sums, relay, landed, zsend, zback, place, gpart,
    wsem, a2a_s, a2a_r, ag_s, ag_r, mate_s, mate_r, rs_s, rs_r, back_s, back_r, gg_s, gg_r,
):
    cols, tok_dev = tok_ref.shape
    zs, per_dev, cap = slots.shape[1:4]
    width, hidden_here = w_in.shape[1:]
    experts = zs * per_dev
    z = lax.axis_index("expert")
    d = lax.axis_index("dp")
    core = d % 2
    xbit = (d // 2) % 2
    ybit = d // 4
    mate_d = d + 1 - 2 * core
    xn = d + 2 - 4 * xbit
    yn = d + 4 - 8 * ybit
    dd = xn + 4 - 8 * ybit
    first = core * yn + (1 - core) * xn
    second = core * xn + (1 - core) * yn

    def remote(src, dst, send, recv, zi, di):
        return pltpu.make_async_remote_copy(
            src_ref=src, dst_ref=dst, send_sem=send, recv_sem=recv, device_id=(zi, di), device_id_type=MESH
        )

    barrier = pltpu.get_barrier_semaphore()
    for step in range(1, zs):
        pl.semaphore_signal(barrier, inc=1, device_id=((z + step) % zs, d), device_id_type=MESH)
    for other in (mate_d, xn, yn):
        pl.semaphore_signal(barrier, inc=1, device_id=(z, other), device_id_type=MESH)

    w_copies = []
    for j in range(per_dev):
        w_copies.append(pltpu.make_async_copy(w_in_hbm.at[j], w_in.at[j], wsem.at[0, j]))
        w_copies.append(pltpu.make_async_copy(w_out_hbm.at[j], w_out.at[j], wsem.at[1, j]))
    for copy in w_copies:
        copy.start()

    named = lax.broadcasted_iota(jnp.int32, (experts, tok_dev), 0)
    first_of = (named == routes_t[0:1, :]).astype(F32)
    second_of = (named == routes_t[1:2, :]).astype(F32)
    before = (
        lax.broadcasted_iota(jnp.int32, (tok_dev, tok_dev), 0)
        < lax.broadcasted_iota(jnp.int32, (tok_dev, tok_dev), 1)
    ).astype(F32).astype(BF16)
    earlier = dot((first_of + second_of).astype(BF16), before, (1, 0))
    slot_iota = lax.broadcasted_iota(jnp.int32, (experts * cap, tok_dev), 0)
    gate_col = jnp.zeros((experts * cap, 1), F32)
    for k, of in ((0, first_of), (1, second_of)):
        rank = jnp.sum(earlier * of, axis=0, keepdims=True).astype(jnp.int32)
        taken = (slot_iota == routes_t[k : k + 1, :] * cap + rank).astype(F32)
        place[k] = taken.astype(BF16)
        gate_col = gate_col + jnp.sum(taken * gates_t[k : k + 1, :], axis=1, keepdims=True)
    both = place[0] + place[1]
    by_slot = (zs, per_dev, cap, cols)
    a2a = [
        [
            [
                remote(
                    slots.at[a, (z + step) % zs, j], zgot.at[a, z, j],
                    a2a_s.at[a, j, step - 1], a2a_r.at[a, j, step - 1], (z + step) % zs, d,
                )
                for step in range(1, zs)
            ]
            for j in range(per_dev)
        ]
        for a in range(2)
    ]

    def exchange(a, j):
        for copy in a2a[a][j]:
            copy.start()

    slots[0] = dot(both, tok_ref[...], (1, 1)).reshape(by_slot).astype(BF16)
    pl.semaphore_wait(barrier, zs + 2)
    exchange(0, 0)
    exchange(0, 1)
    zgot[0, pl.ds(z, 1)] = slots[0, pl.ds(z, 1)]
    slots[1] = (dot(both, cot_ref[...], (1, 1)) * gate_col).reshape(by_slot).astype(BF16)
    zgot[1, pl.ds(z, 1)] = slots[1, pl.ds(z, 1)]

    def ag_copy(a, j, i):
        block, to = (
            (d, xn), (d, yn), (d, mate_d),
            (second, first), (xn, mate_d), (yn, mate_d), (dd, mate_d),
        )[i]
        here = gath.at[a, j, block]
        return remote(here, here, ag_s.at[a, j, i], ag_r.at[a, j, i], z, to)

    ag = [[[ag_copy(a, j, i) for i in range(7)] for j in range(per_dev)] for a in range(2)]

    def arrive(a, j):
        for copy in a2a[a][j]:
            copy.wait()

    def assemble(a, j):
        whole = jnp.concatenate([zgot[a, i, j].astype(F32) for i in range(zs)], axis=-1)
        gath[a, j, pl.ds(d, 1)] = whole.astype(BF16)[None]
        for i in range(3):
            ag[a][j][i].start()

    def forward(a, j):
        ag[a][j][0].wait_recv()
        ag[a][j][1].wait_recv()
        for i in (3, 4, 5):
            ag[a][j][i].start()

    def forward_last(a, j):
        ag[a][j][3].wait_recv()
        ag[a][j][6].start()

    def finish(a, j):
        for i in (2, 4, 5, 6):
            ag[a][j][i].wait_recv()

        def column(n, carry):
            at = pl.ds(pl.multiple_of(n * 128, 128), 128)
            blocks = [gath[a, j, 2 * chip + half, :, at].astype(F32) for half in range(2) for chip in range(4)]
            rows[a, j, :, at] = jnp.concatenate(blocks, axis=0).astype(BF16)
            return carry

        lax.fori_loop(0, width // 128, column, 0)

    def activation(j):
        def column(n, carry):
            at = pl.ds(pl.multiple_of(n * 256, 256), 256)
            v = dot(rows[0, j], w_in[j, :, at], (1, 0))
            scale = 0.7978845608028654
            sq = v * v
            t = jnp.tanh(scale * v * (1.0 + 0.044715 * sq))
            half = 0.5 * (1.0 + t)
            hid[j, :, at] = (v * half).astype(BF16)
            slope[j, :, at] = half + 0.5 * v * (1.0 - t * t) * (scale * (1.0 + 0.134145 * sq))
            return carry

        lax.fori_loop(0, hidden_here // 256, column, 0)

    def backward(j):
        def column(n, carry):
            at = pl.ds(pl.multiple_of(n * 256, 256), 256)
            dh = dot(rows[1, j], w_out[j, at, :], (1, 1))
            dpre[j, :, at] = (slope[j, :, at] * dh).astype(BF16)
            return carry

        lax.fori_loop(0, hidden_here // 256, column, 0)

    def mate_copy(a, j):
        return remote(
            term.at[a, j, 1 - core], mate.at[a, j], mate_s.at[a, j], mate_r.at[a, j], z, mate_d
        )

    mates = [[mate_copy(a, j) for j in range(per_dev)] for a in range(2)]

    def terms(a, j):
        for lo, size in tiles_of(width):
            if a == 0:
                v = dot(hid[j], w_out[j, :, lo : lo + size], (1, 0))
            else:
                v = dot(dpre[j], w_in[j, lo : lo + size, :], (1, 1))
            term[a, j, :, :, :, lo : lo + size] = v.reshape(2, 4, cap, size).astype(BF16)
        mates[a][j].start()

    def rs_copy(a, j, i):
        src, to = (
            (sums.at[a, j, dd // 2], first), (sums.at[a, j, first // 2], first), (relay.at[a, j], second)
        )[i]
        return remote(src, landed.at[a, j, i], rs_s.at[a, j, i], rs_r.at[a, j, i], z, to)

    rs = [[[rs_copy(a, j, i) for i in range(3)] for j in range(per_dev)] for a in range(2)]

    def rs_start(a, j):
        mates[a][j].wait()

        def column(n, carry):
            at = pl.ds(pl.multiple_of(n * 128, 128), 128)
            both_cores = term[a, j, core, :, :, at].astype(F32) + mate[a, j, :, :, at].astype(F32)
            sums[a, j, :, :, at] = both_cores.astype(BF16)
            return carry

        lax.fori_loop(0, width // 128, column, 0)
        rs[a][j][0].start()
        rs[a][j][1].start()

    def rs_relay(a, j):
        rs[a][j][0].wait()
        relay[a, j] = (sums[a, j, second // 2].astype(F32) + landed[a, j, 0].astype(F32)).astype(BF16)
        rs[a][j][2].start()

    def back_copy(a, j, step):
        to = (z + step) % zs
        return remote(
            zsend.at[a, to, j], zback.at[a, z, j],
            back_s.at[a, j, step - 1], back_r.at[a, j, step - 1], to, d,
        )

    back = [
        [[back_copy(a, j, step) for step in range(1, zs)] for j in range(per_dev)] for a in range(2)
    ]

    def rs_end(a, j):
        rs[a][j][1].wait()
        rs[a][j][2].wait()
        total = sums[a, j, d // 2].astype(F32) + landed[a, j, 1].astype(F32) + landed[a, j, 2].astype(F32)
        for i in range(zs):
            zsend[a, i, j] = total[:, i * cols : (i + 1) * cols].astype(BF16)
        for copy in back[a][j]:
            copy.start()
        zback[a, pl.ds(z, 1), j] = zsend[a, pl.ds(z, 1), j]

    def weight_grad_out(j):
        def part(m, carry):
            at = pl.ds(pl.multiple_of(m * 256, 256), 256)
            left = hid[j, :, at]
            for lo, size in tiles_of(width):
                go[j, at, lo : lo + size] = dot(left, rows[1, j, :, lo : lo + size], (0, 0)).astype(BF16)
            return carry

        lax.fori_loop(0, hidden_here // 256, part, 0)

    def weight_grad_in(j):
        def part(m, carry):
            at = pl.ds(pl.multiple_of(m * 128, 128), 128)
            gi[j, at, :] = dot(rows[0, j, :, at], dpre[j], (0, 0)).astype(BF16)
            return carry

        lax.fori_loop(0, width // 128, part, 0)

    gg = []
    for step in range(1, zs):
        gg.append(
            remote(
                gpart.at[z], gpart.at[z], gg_s.at[step - 1], gg_r.at[step - 1], (z + step) % zs, d
            )
        )

    def combine(a):
        for j in range(per_dev):
            for copy in back[a][j]:
                copy.wait()
        slot_rows = zback[a].astype(F32).reshape(experts * cap, cols).astype(BF16)
        views = [dot(slot_rows, place[k], (0, 0)) for k in range(2)]
        if a == 1:
            gtok_ref[...] = (views[0] + views[1]).astype(BF16)
            return
        out_ref[...] = (views[0] * gates_t[0:1, :] + views[1] * gates_t[1:2, :]).astype(BF16)
        cot = cot_ref[...].astype(F32)
        inner = [jnp.sum(cot * v, axis=0, keepdims=True) for v in views]
        row = lax.broadcasted_iota(jnp.int32, (8, tok_dev), 0)
        gpart[pl.ds(z, 1)] = jnp.where(row == 0, inner[0], inner[1])[None]
        for copy in gg:
            copy.start()

    arrive(0, 0)
    assemble(0, 0)
    arrive(0, 1)
    exchange(1, 0)
    exchange(1, 1)
    assemble(0, 1)
    forward(0, 0)
    arrive(1, 0)
    assemble(1, 0)
    forward(0, 1)
    forward_last(0, 0)
    arrive(1, 1)
    assemble(1, 1)
    for copy in w_copies:
        copy.wait()
    finish(0, 0)
    forward_last(0, 1)
    activation(0)
    forward(1, 0)
    terms(0, 0)
    forward_last(1, 0)
    forward(1, 1)
    finish(0, 1)
    activation(1)
    rs_start(0, 0)
    forward_last(1, 1)
    terms(0, 1)
    finish(1, 0)
    backward(0)
    rs_start(0, 1)
    terms(1, 0)
    rs_relay(0, 0)
    finish(1, 1)
    backward(1)
    rs_start(1, 0)
    rs_relay(0, 1)
    terms(1, 1)
    rs_end(0, 0)
    rs_relay(1, 0)
    rs_end(0, 1)
    weight_grad_out(0)
    rs_start(1, 1)
    weight_grad_out(1)
    rs_end(1, 0)
    rs_relay(1, 1)
    combine(0)
    weight_grad_in(0)
    rs_end(1, 1)
    weight_grad_in(1)
    for copy in gg:
        copy.wait()
    total = gpart[0] + gpart[1] + gpart[2] + gpart[3]
    gg_ref[...] = total[0:2]
    combine(1)
    for a in range(2):
        for j in range(per_dev):
            for copy in ag[a][j]:
                copy.wait_send()


def fused_shards(tokens, routes, gate_values, expert_in, expert_out, cotangent):
    tok_dev, cols = tokens.shape
    zs = lax.axis_size("expert")
    dps = lax.axis_size("dp")
    per_dev, width, hidden_here = expert_in.shape
    experts = per_dev * zs
    cap = 5 * tok_dev // (2 * experts)
    all_rows = dps * cap
    vmem = pl.BlockSpec(memory_space=pltpu.VMEM)
    hbm = pl.BlockSpec(memory_space=pl.ANY)
    dma = pltpu.SemaphoreType.DMA
    layer_t, gtok_t, gates_grad_t, grad_in, grad_out = pl.pallas_call(
        layer_kernel,
        out_shape=(
            pltpu.VMEM((cols, tok_dev), BF16),
            pltpu.VMEM((cols, tok_dev), BF16),
            pltpu.VMEM((2, tok_dev), F32),
            pltpu.VMEM(expert_in.shape, BF16),
            pltpu.VMEM(expert_out.shape, BF16),
        ),
        in_specs=[vmem] * 4 + [hbm] * 2,
        out_specs=(vmem,) * 5,
        scratch_shapes=[
            pltpu.VMEM(expert_in.shape, BF16),
            pltpu.VMEM(expert_out.shape, BF16),
            pltpu.VMEM((2, zs, per_dev, cap, cols), BF16),
            pltpu.VMEM((2, zs, per_dev, cap, cols), BF16),
            pltpu.VMEM((2, per_dev, dps, cap, width), BF16),
            pltpu.VMEM((2, per_dev, all_rows, width), BF16),
            pltpu.VMEM((per_dev, all_rows, hidden_here), BF16),
            pltpu.VMEM((per_dev, all_rows, hidden_here), F32),
            pltpu.VMEM((per_dev, all_rows, hidden_here), BF16),
            pltpu.VMEM((2, per_dev, 2, dps // 2, cap, width), BF16),
            pltpu.VMEM((2, per_dev, dps // 2, cap, width), BF16),
            pltpu.VMEM((2, per_dev, dps // 2, cap, width), BF16),
            pltpu.VMEM((2, per_dev, cap, width), BF16),
            pltpu.VMEM((2, per_dev, 3, cap, width), BF16),
            pltpu.VMEM((2, zs, per_dev, cap, cols), BF16),
            pltpu.VMEM((2, zs, per_dev, cap, cols), BF16),
            pltpu.VMEM((2, experts * cap, tok_dev), BF16),
            pltpu.VMEM((zs, 8, tok_dev), F32),
            dma((2, per_dev)),
            dma((2, per_dev, zs - 1)), dma((2, per_dev, zs - 1)),
            dma((2, per_dev, 7)), dma((2, per_dev, 7)),
            dma((2, per_dev)), dma((2, per_dev)),
            dma((2, per_dev, 3)), dma((2, per_dev, 3)),
            dma((2, per_dev, zs - 1)), dma((2, per_dev, zs - 1)),
            dma((zs - 1,)), dma((zs - 1,)),
        ],
        compiler_params=pltpu.CompilerParams(
            collective_id=0, has_side_effects=True, vmem_limit_bytes=46 * 1024 * 1024
        ),
    )(tokens.T, cotangent.T, routes.T, gate_values.T, expert_in, expert_out)
    return (layer_t.T, gtok_t.T, gates_grad_t.T, grad_in, grad_out)


def solution(mesh):
    placed = (
        P("dp", "expert"),
        P("dp", None),
        P("dp", None),
        P("expert", None, "dp"),
        P("expert", "dp", None),
        P("dp", "expert"),
    )
    fused = mesh.shape["expert"] == 4 and mesh.shape["dp"] == 8
    return jax.shard_map(
        fused_shards if fused else shards,
        mesh=mesh,
        in_specs=placed,
        out_specs=(
            P("dp", "expert"),
            P("dp", "expert"),
            P("dp", None),
            P("expert", None, "dp"),
            P("expert", "dp", None),
        ),
        check_vma=False,
    )
```
